32 devices in a mesh: expert: 8 (over z, y), dp: 4 (over x, core).
Axes of the slice: x: 2, y: 2, z: 4, core: 2. Of those that a mesh axis runs over, the one named last changes fastest.
Arguments:
- tokens: bfloat16 [4096, 4096], P(('expert', 'dp')), may hold values from -6 to 6
- expert_ids: int32 [4096, 2], P(('expert', 'dp')), may hold values from 0 to 15, all different within a row; in each aligned block of 128 rows (0 to 127, 128 to 255, ...) at most 48 rows name the same one
- gate_codes: int32 [4096, 2], P(('expert', 'dp')), may hold values from 1 to 255
- first_shared: bfloat16 [64, 64, 64], P('dp'), may hold values from -0.75 to 0.75
- second_shared: bfloat16 [64, 64, 256], P('dp'), may hold values from -0.75 to 0.75
- third_shared: bfloat16 [64, 256, 64], P('dp'), may hold values from -0.375 to 0.375
- fourth_shared: bfloat16 [64, 64, 64], P('dp'), may hold values from -0.75 to 0.75
- first_routed: bfloat16 [16, 64, 64, 64], P('expert'), may hold values from -0.75 to 0.75
- second_routed: bfloat16 [16, 64, 64, 256], P('expert'), may hold values from -0.75 to 0.75
- third_routed: bfloat16 [16, 64, 256, 64], P('expert'), may hold values from -0.375 to 0.375
- fourth_routed: bfloat16 [16, 64, 64, 64], P('expert'), may hold values from -0.75 to 0.75
Outputs:
- mixed: bfloat16 [4096, 4096], P(('expert', 'dp'))
The draws below stay inside these ranges and needn't reach their ends.
Inputs may be any that keep to these rules, and one draw needn't show every extreme that they name: `expert_ids`: each token names two different experts; among the 128 tokens of one device no expert is named more than 48 times.
All inputs are finite; a program needn't handle non-finite values.
Results may differ from the reference program's by a relative error of at most 0.0075.
Values may be sent and summed in bfloat16 or wider, within the bound.
A program may use at most 128 MiB of HBM per device.

```python
import math
import jax
import jax.numpy as jnp
import numpy as np
from jax import lax

D = 4096
NB = 64
DB = 64
HB = 256
EXPERTS = 16
TOK_DEV = 128
TOKENS = 4096
MOST = 48


def set_ends(drawn, own_key, least, top_value):
    extent = drawn.shape
    index_at = [jax.random.randint(jax.random.fold_in(own_key, axis), (), 0, extent[axis]) for axis in range(len(extent))]
    drawn = drawn.at[tuple(index_at)].set(least)
    longest = extent.index(max(extent))
    index_at[longest] = (index_at[longest] + 1) % extent[longest]
    return drawn.at[tuple(index_at)].set(top_value)


def block_scale(own_key, dims, shards, low, top_value):
    gain, own = 1.0, jax.random.fold_in(own_key, 6)
    for dim, blocks in shards:
        heights = jnp.exp(jax.random.uniform(jax.random.fold_in(own, dim), (blocks,), jnp.float32, low / len(shards), top_value / len(shards)))
        gain = gain * jnp.repeat(heights, dims[dim] // blocks).reshape([-1 if axis == dim else 1 for axis in range(len(dims))])
    return gain


def deal_out(stream_key, own, number, rows, number_of, top, limit, lean):
    order = jax.random.permutation(stream_key, number_of)
    packed, ordinary = portions_of(number_of, rows * top, limit, lean, True), portions_of(number_of, rows * top, limit, lean, False)
    places = jnp.arange(number_of)

    def named(lengths, rotation):
        used = int((lengths > 0).sum())
        fixed = max(1, used // 4)
        shifted = fixed + (places - fixed + rotation * (used - fixed)) % max(1, number_of - fixed)
        return jnp.zeros((number_of,), jnp.int32).at[order[jnp.where(places < fixed, places, shifted)]].set(jnp.asarray(lengths, jnp.int32))

    lengths = jnp.where(number % 4 == 0, named(packed, number // 4), named(ordinary, number - number // 4 - 1))
    mixed = jax.random.permutation(jax.random.fold_in(own, 3), number_of)
    donor, taker = mixed[0:number_of // 2 * 2:2], mixed[1:number_of // 2 * 2:2]
    room = jnp.minimum(lengths[donor] - 1, limit - lengths[taker]) // 2
    room = jnp.where((donor == order[0]) | (taker == order[0]) | (lengths[taker] == 0), 0, jnp.maximum(room, 0))
    shifted = jax.random.randint(jax.random.fold_in(own, 4), (number_of // 2,), 0, 1 << 20) % (room + 1)
    lengths = lengths.at[donor].add(-shifted).at[taker].add(shifted)
    labels = jnp.searchsorted(jnp.cumsum(lengths), jnp.arange(rows * top), side="right").astype(jnp.int32)
    listing = labels.reshape(top, rows).T
    listing = listing[jax.random.permutation(jax.random.fold_in(own, 1), rows)]
    rotation = jax.random.randint(jax.random.fold_in(own, 2), (rows, 1), 0, top)
    return jnp.take_along_axis(listing, (jnp.arange(top)[None, :] + rotation) % top, axis=1)


def portions_of(count, total, reach, lean, full):
    portions = [(1 << 20) // math.isqrt(standing ** lean) + 1 for standing in range(1, count + 1)]
    largest = reach if full else min(reach, max(-(-total // count), total * portions[0] // sum(portions)))
    least = 1 if total - largest >= count - 1 else 0
    given, spare = [largest] + [least] * (count - 1), total - largest - least * (count - 1)
    while spare > 0:
        free = [i for i in range(1, count) if given[i] < largest] or [i for i in range(1, count) if given[i] < reach]
        pool, remaining = sum([portions[i] for i in free]), spare
        for i in free:
            extra = min(reach - given[i], max(1, remaining * portions[i] // pool), spare)
            given[i] = given[i] + extra
            spare = spare - extra
    return np.array(given)


def centred(own_key, dims, spread, reach, shards=(), held_as=jnp.bfloat16):
    loudness = block_scale(own_key, dims, shards, -0.22, 0.18) if shards else 1.0
    values = jax.random.normal(own_key, dims, jnp.float32) * spread * loudness
    return jnp.minimum(jnp.maximum(values, -reach), reach).astype(held_as)


def setup_inputs(seed: int = 0) -> dict:
    seeds = jax.random.split(jax.random.key(seed), 12)
    tokens = centred(seeds[0], (TOKENS, D), 1.0, 6.0, ((0, 32),))
    expert_ids_keys = jax.random.split(jax.random.fold_in(seeds[1], 1), TOKENS // TOK_DEV)
    expert_ids_turns = jax.random.permutation(jax.random.fold_in(seeds[1], 3), TOKENS // TOK_DEV)
    expert_ids = jax.vmap(lambda own, number: deal_out(jax.random.fold_in(seeds[1], 2), own, number, TOK_DEV, EXPERTS, 2, MOST, 2))(expert_ids_keys, expert_ids_turns).reshape((TOKENS, 2))
    gate_codes = set_ends(jax.random.randint(seeds[2], (TOKENS, 2), 1, 256), jax.random.fold_in(seeds[2], 1), 1, 255).astype(jnp.int32)
    first_shared = centred(seeds[3], (NB, DB, NB), DB ** -0.5, 0.75, ((0, 4),))
    second_shared = centred(seeds[4], (NB, NB, HB), NB ** -0.5, 0.75, ((0, 4),))
    third_shared = centred(seeds[5], (NB, HB, NB), HB ** -0.5, 0.375, ((0, 4),))
    fourth_shared = centred(seeds[6], (NB, NB, DB), NB ** -0.5, 0.75, ((0, 4),))
    first_routed = centred(seeds[7], (EXPERTS, NB, DB, NB), DB ** -0.5, 0.75, ((0, 8),))
    second_routed = centred(seeds[8], (EXPERTS, NB, NB, HB), NB ** -0.5, 0.75, ((0, 8),))
    third_routed = centred(seeds[9], (EXPERTS, NB, HB, NB), HB ** -0.5, 0.375, ((0, 8),))
    fourth_routed = centred(seeds[10], (EXPERTS, NB, NB, DB), NB ** -0.5, 0.75, ((0, 8),))
    return dict(tokens=tokens, expert_ids=expert_ids, gate_codes=gate_codes, first_shared=first_shared, second_shared=second_shared, third_shared=third_shared, fourth_shared=fourth_shared, first_routed=first_routed, second_routed=second_routed, third_routed=third_routed, fourth_routed=fourth_routed)


row_block = 512


def expand(rows, first, second):
    blocks = rows.reshape(rows.shape[0], NB, DB).astype(jnp.float32)
    first_out = jnp.einsum("rab,abj->raj", blocks, first.astype(jnp.float32)).astype(jnp.bfloat16)
    first_out = lax.optimization_barrier(first_out)
    hidden = jnp.einsum("raj,jac->rjc", first_out.astype(jnp.float32), second.astype(jnp.float32))
    return jax.nn.gelu(hidden, approximate=False).astype(jnp.bfloat16)


def contract(hidden, third, fourth):
    hidden = lax.optimization_barrier(hidden)
    inner = jnp.einsum("rjc,jck->rjk", hidden.astype(jnp.float32), third.astype(jnp.float32)).astype(jnp.bfloat16)
    inner = lax.optimization_barrier(inner)
    output = jnp.einsum("rjk,kjm->rkm", inner.astype(jnp.float32), fourth.astype(jnp.float32))
    return output.reshape(output.shape[0], D).astype(jnp.bfloat16)


def monarch(rows, factors):
    return contract(expand(rows, factors[0], factors[1]), factors[2], factors[3])


def reference(tokens, expert_ids, gate_codes, first_shared, second_shared, third_shared, fourth_shared,
              first_routed, second_routed, third_routed, fourth_routed):
    shared = (first_shared, second_shared, third_shared, fourth_shared)
    routed = (first_routed, second_routed, third_routed, fourth_routed)
    blocksize = math.gcd(TOKENS, row_block)

    def shared_block(rows):
        return monarch(rows, shared)

    shared_out = lax.map(shared_block, tokens.reshape(TOKENS // blocksize, blocksize, D)).reshape(TOKENS, D)

    picks = expert_ids.reshape(-1).astype(jnp.int32)
    pair_count = picks.shape[0]
    ordering = jnp.argsort(picks, stable=True).astype(jnp.int32)
    counts = jnp.sum((picks[:, None] == jnp.arange(EXPERTS, dtype=jnp.int32)[None, :]).astype(jnp.int32), axis=0)
    starts = (jnp.cumsum(counts) - counts).astype(jnp.int32)
    padded_order = jnp.concatenate([ordering, jnp.zeros((row_block,), jnp.int32)])
    outputs = jnp.zeros((pair_count, D), jnp.bfloat16)

    def expert_step(number, outputs):
        factors = tuple(lax.dynamic_index_in_dim(weight, number, 0, keepdims=False) for weight in routed)
        begin = starts[number]
        amount = counts[number]
        nblocks = (amount + row_block - 1) // row_block

        def block_step(position, outputs):
            offset = (begin + position * row_block).astype(jnp.int32)
            indexes = lax.dynamic_slice_in_dim(padded_order, offset, row_block)
            valid = (offset + jnp.arange(row_block, dtype=jnp.int32)) < begin + amount
            rows = tokens[indexes // 2]
            values = monarch(rows, factors)
            target = jnp.where(valid, indexes, pair_count).astype(jnp.int32)
            return outputs.at[target].set(values, mode="drop")

        return lax.fori_loop(0, nblocks, block_step, outputs)

    outputs = lax.fori_loop(0, EXPERTS, expert_step, outputs)
    routed_out = outputs.reshape(TOKENS, 2, D).astype(jnp.float32)
    codes = gate_codes.astype(jnp.float32)
    gates = codes / jnp.sum(codes, axis=1, keepdims=True)
    total = shared_out.astype(jnp.float32) + gates[:, 0:1] * routed_out[:, 0] + gates[:, 1:2] * routed_out[:, 1]
    return total.astype(jnp.bfloat16)
```

```python
import functools

import jax
import jax.numpy as jnp
from jax import lax
from jax.experimental import pallas as pl
from jax.experimental.pallas import tpu as pltpu
from jax.sharding import PartitionSpec as P

D = 4096
NB = 64
DB = 64
HB = 256
T = 128
F32 = jnp.float32
BF16 = jnp.bfloat16


def tile_monarch(x_tile, w1_ref, w2_ref, w3_ref, w4_ref, z_ref, u_ref, store):
    def up(a, carry):
        rows = pl.ds(pl.multiple_of(a * DB, DB), DB)
        z = jnp.dot(w1_ref[0, a], x_tile[rows, :], preferred_element_type=F32)
        z_ref[rows, :] = z
        return carry

    lax.fori_loop(0, NB, up, 0, unroll=8)

    def middle(j, carry):
        z = z_ref[pl.ds(j, NB, stride=NB), :].astype(BF16)
        hidden = jnp.dot(w2_ref[0, j], z, preferred_element_type=F32)
        hidden = (0.5 * hidden) * (1.0 + lax.erf(hidden * (0.5**0.5)))
        u = jnp.dot(w3_ref[0, j], hidden.astype(BF16), preferred_element_type=F32)
        u_ref[pl.ds(pl.multiple_of(j * NB, NB), NB), :] = u
        return carry

    lax.fori_loop(0, NB, middle, 0, unroll=4)

    def down(k, carry):
        u = u_ref[pl.ds(k, NB, stride=NB), :].astype(BF16)
        store(k, jnp.dot(w4_ref[0, k], u, preferred_element_type=F32))
        return carry

    lax.fori_loop(0, NB, down, 0, unroll=8)


def shared_kernel(x_ref, w1_ref, w2_ref, w3_ref, w4_ref, o_ref, z_ref, u_ref):
    def store(k, value):
        o_ref[pl.ds(pl.multiple_of(k * DB, DB), DB), :] = value.astype(BF16)

    tile_monarch(x_ref, w1_ref, w2_ref, w3_ref, w4_ref, z_ref, u_ref, store)


def routed_kernel(
    tiles, counts_ref, pos_ref, gate_ref, x_ref, w1_ref, w2_ref, w3_ref, w4_ref,
    o_ref, x_scr, z_ref, u_ref,
):
    expert, tile = pl.program_id(0), pl.program_id(1)
    live = tile * T < counts_ref[expert]
    sources = x_ref.shape[0]

    @pl.when(jnp.logical_not(live))
    def _():
        o_ref[...] = jnp.zeros_like(o_ref)

    @pl.when(live)
    def _():
        wanted = lax.broadcasted_iota(jnp.int32, (T, 2 * T), 0) + tile * T
        quarter = D // 4

        for part in range(4):
            rows = pl.ds(part * quarter, quarter)

            def pick(pair, total):
                both = jnp.concatenate([x_ref[2 * pair, rows, :], x_ref[2 * pair + 1, rows, :]], axis=1)
                onehot = (wanted == pos_ref[0, pair, :, :]).astype(F32).astype(BF16)
                return total + lax.dot_general(
                    both, onehot, (((1,), (1,)), ((), ())), preferred_element_type=F32
                )

            total = lax.fori_loop(0, sources // 2, pick, jnp.zeros((quarter, T), F32))
            x_scr[rows, :] = total.astype(BF16)

        gate = gate_ref[0, 0]

        def store(k, value):
            o_ref[pl.ds(pl.multiple_of(k * DB, DB), DB), :] = (value * gate).astype(BF16)

        tile_monarch(x_scr, w1_ref, w2_ref, w3_ref, w4_ref, z_ref, u_ref, store)


def weight_specs(index_map):
    return [
        pl.BlockSpec((1, NB, NB, DB), index_map),
        pl.BlockSpec((1, NB, HB, NB), index_map),
        pl.BlockSpec((1, NB, NB, HB), index_map),
        pl.BlockSpec((1, NB, DB, NB), index_map),
    ]


def turned(factors):
    return tuple(jnp.swapaxes(w, -1, -2) for w in factors)


def shared_call(x_t, factors):
    return pl.pallas_call(
        shared_kernel,
        out_shape=jax.ShapeDtypeStruct((D, T), BF16),
        grid=(1,),
        in_specs=[pl.BlockSpec((D, T), lambda i: (0, 0))] + weight_specs(lambda i: (0, 0, 0, 0)),
        out_specs=pl.BlockSpec((D, T), lambda i: (0, 0)),
        scratch_shapes=[pltpu.VMEM((D, T), F32), pltpu.VMEM((D, T), F32)],
        compiler_params=pltpu.CompilerParams(vmem_limit_bytes=56 * 2**20),
        cost_estimate=pl.CostEstimate(flops=10**10, bytes_accessed=10**7, transcendentals=0),
        name="shared_expert",
    )(x_t, *factors)


def routed_call(counts, pos, slot_gates, x_all, factors, tiles):
    residents = pos.shape[0]
    sources = x_all.shape[0]
    grid_spec = pltpu.PrefetchScalarGridSpec(
        num_scalar_prefetch=1,
        grid=(residents, tiles),
        in_specs=[
            pl.BlockSpec((1, sources // 2, 1, 2 * T), lambda e, i, c: (e, 0, 0, 0)),
            pl.BlockSpec((1, 1, 1, T), lambda e, i, c: (e, i, 0, 0)),
            pl.BlockSpec((sources, D, T), lambda e, i, c: (0, 0, 0), pipeline_mode=pl.Buffered(1)),
        ]
        + weight_specs(lambda e, i, c: (e, 0, 0, 0)),
        out_specs=pl.BlockSpec((D, T), lambda e, i, c: (0, e * tiles + i)),
        scratch_shapes=[pltpu.VMEM((D, T), BF16), pltpu.VMEM((D, T), F32), pltpu.VMEM((D, T), F32)],
    )
    return pl.pallas_call(
        functools.partial(routed_kernel, tiles),
        out_shape=jax.ShapeDtypeStruct((D, residents * tiles * T), BF16),
        grid_spec=grid_spec,
        compiler_params=pltpu.CompilerParams(vmem_limit_bytes=62 * 2**20),
        cost_estimate=pl.CostEstimate(flops=4 * 10**10, bytes_accessed=2 * 10**7, transcendentals=0),
        name="routed_experts",
    )(counts, pos, slot_gates, x_all, *factors)


def combine_kernel(tiles, counts_ref, pos_ref, o_ref, y_ref, acc_ref):
    residents = counts_ref.shape[0]
    depth = tiles * T
    wanted = lax.broadcasted_iota(jnp.int32, (depth, 2 * T), 0)
    hots = [(wanted == pos_ref[e, 0, :, :]).astype(F32).astype(BF16) for e in range(residents)]
    hot = jnp.concatenate(hots, axis=0)
    step = 512

    def part(i, carry):
        rows = pl.ds(pl.multiple_of(i * step, step), step)
        total = jnp.dot(o_ref[rows, :], hot, preferred_element_type=F32).astype(BF16)
        y_ref[0, rows, :] = total[:, :T]
        y_ref[1, rows, :] = total[:, T:]
        return carry

    lax.fori_loop(0, D // step, part, 0)


def combine_call(counts, pos, outs, sources, tiles):
    residents = pos.shape[0]
    grid_spec = pltpu.PrefetchScalarGridSpec(
        num_scalar_prefetch=1,
        grid=(sources // 2,),
        in_specs=[
            pl.BlockSpec((residents, 1, 1, 2 * T), lambda s, c: (0, s, 0, 0)),
            pl.BlockSpec((D, residents * tiles * T), lambda s, c: (0, 0), pipeline_mode=pl.Buffered(1)),
        ],
        out_specs=pl.BlockSpec((2, D, T), lambda s, c: (s, 0, 0)),
        scratch_shapes=[pltpu.VMEM((8, T), F32)],
    )
    return pl.pallas_call(
        functools.partial(combine_kernel, tiles),
        out_shape=jax.ShapeDtypeStruct((sources, D, T), BF16),
        grid_spec=grid_spec,
        compiler_params=pltpu.CompilerParams(vmem_limit_bytes=48 * 2**20),
        name="combine",
    )(counts, pos, outs)


def gather_tokens(x_t):
    return lax.all_gather(x_t, "expert", axis=0, tiled=False)


def scatter_sums(y):
    return lax.psum_scatter(y, "expert", scatter_dimension=0, tiled=False)


def shards(tokens, expert_ids, gate_codes, *factors):
    shared, routed = factors[:4], factors[4:]
    residents = routed[0].shape[0]
    sources = lax.axis_size("expert")
    tok_rows = tokens.shape[0]
    experts_all = residents * sources
    capacity = max(2, 6 * tok_rows // experts_all)
    tiles = -(-sources * capacity // T)

    x_t = tokens.T
    x_all = gather_tokens(x_t)
    codes = gate_codes.astype(F32)
    gates = codes / jnp.sum(codes, axis=1, keepdims=True)
    ids_all = lax.all_gather(expert_ids.T, "expert", axis=0)
    gates_all = lax.all_gather(gates.T, "expert", axis=0)
    mine = lax.axis_index("expert") * residents + jnp.arange(residents, dtype=jnp.int32)
    match = ids_all[None] == mine[:, None, None, None]
    picked = jnp.any(match, axis=2).reshape(residents, sources * tok_rows)
    gate = jnp.sum(jnp.where(match, gates_all[None], 0.0), axis=2).reshape(residents, sources * tok_rows)
    ones = picked.astype(jnp.int32)
    ranks = jnp.cumsum(ones, axis=1)
    counts = ranks[:, -1]
    pos = jnp.where(picked, ranks - 1, -1)
    slots = jnp.arange(tiles * T, dtype=jnp.int32)
    slot_gates = jnp.sum(
        jnp.where(pos[:, None, :] == slots[None, :, None], gate[:, None, :], 0.0), axis=2
    ).reshape(residents, tiles, 1, T)
    pos = pos.reshape(residents, sources // 2, 1, 2 * T)

    outs = routed_call(counts, pos, slot_gates, x_all, turned(routed), tiles)
    y = combine_call(counts, pos, outs, sources, tiles)
    sums = scatter_sums(y)
    whole = tuple(lax.all_gather(w, "dp", axis=0, tiled=True)[None] for w in turned(shared))
    shared_t = shared_call(x_t, whole)
    total = shared_t.astype(F32) + sums.astype(F32)
    return total.astype(BF16).T


def solution(mesh):
    in_specs = (
        P(("expert", "dp"), None),
        P(("expert", "dp"), None),
        P(("expert", "dp"), None),
        P("dp", None, None),
        P("dp", None, None),
        P("dp", None, None),
        P("dp", None, None),
        P("expert", None, None, None),
        P("expert", None, None, None),
        P("expert", None, None, None),
        P("expert", None, None, None),
    )
    out_specs = P(("expert", "dp"), None)
    return jax.shard_map(shards, mesh=mesh, in_specs=in_specs, out_specs=out_specs, check_vma=False)
```

```python
import functools
import math

import jax
import jax.numpy as jnp
from jax import lax
from jax.experimental import pallas as pl
from jax.experimental.pallas import tpu as pltpu
from jax.sharding import PartitionSpec as P

D = 4096
NB = 64
DB = 64
HB = 256
T = 128
F32 = jnp.float32
BF16 = jnp.bfloat16


def tile_monarch(x_tile, w1_ref, w2_ref, w3_ref, w4_ref, z_ref, u_ref, store):
    def up(a, carry):
        rows = pl.ds(pl.multiple_of(a * DB, DB), DB)
        z = jnp.dot(w1_ref[0, a], x_tile[rows, :], preferred_element_type=F32)
        z_ref[rows, :] = z
        return carry

    lax.fori_loop(0, NB, up, 0, unroll=8)

    def middle(j, carry):
        z = z_ref[pl.ds(j, NB, stride=NB), :].astype(BF16)
        hidden = jnp.dot(w2_ref[0, j], z, preferred_element_type=F32)
        hidden = (0.5 * hidden) * (1.0 + lax.erf(hidden * (0.5**0.5)))
        u = jnp.dot(w3_ref[0, j], hidden.astype(BF16), preferred_element_type=F32)
        u_ref[pl.ds(pl.multiple_of(j * NB, NB), NB), :] = u
        return carry

    lax.fori_loop(0, NB, middle, 0, unroll=4)

    def down(k, carry):
        u = u_ref[pl.ds(k, NB, stride=NB), :].astype(BF16)
        store(k, jnp.dot(w4_ref[0, k], u, preferred_element_type=F32))
        return carry

    lax.fori_loop(0, NB, down, 0, unroll=8)


def shared_kernel(x_ref, w1_ref, w2_ref, w3_ref, w4_ref, o_ref, z_ref, u_ref):
    def store(k, value):
        o_ref[pl.ds(pl.multiple_of(k * DB, DB), DB), :] = value.astype(BF16)

    tile_monarch(x_ref, w1_ref, w2_ref, w3_ref, w4_ref, z_ref, u_ref, store)


def routed_kernel(
    tiles, counts_ref, pos_ref, gate_ref, x_ref, w1_ref, w2_ref, w3_ref, w4_ref,
    o_ref, x_scr, z_ref, u_ref,
):
    expert, tile = pl.program_id(0), pl.program_id(1)
    live = tile * T < counts_ref[expert]
    sources = x_ref.shape[0]

    @pl.when(jnp.logical_not(live))
    def _():
        o_ref[...] = jnp.zeros_like(o_ref)

    @pl.when(live)
    def _():
        wanted = lax.broadcasted_iota(jnp.int32, (T, 2 * T), 0) + tile * T
        quarter = D // 4

        for part in range(4):
            rows = pl.ds(part * quarter, quarter)

            def pick(pair, total):
                both = jnp.concatenate([x_ref[2 * pair, rows, :], x_ref[2 * pair + 1, rows, :]], axis=1)
                onehot = (wanted == pos_ref[0, pair, :, :]).astype(F32).astype(BF16)
                return total + lax.dot_general(
                    both, onehot, (((1,), (1,)), ((), ())), preferred_element_type=F32
                )

            total = lax.fori_loop(0, sources // 2, pick, jnp.zeros((quarter, T), F32))
            x_scr[rows, :] = total.astype(BF16)

        gate = gate_ref[0, 0]

        def store(k, value):
            o_ref[pl.ds(pl.multiple_of(k * DB, DB), DB), :] = (value * gate).astype(BF16)

        tile_monarch(x_scr, w1_ref, w2_ref, w3_ref, w4_ref, z_ref, u_ref, store)


def weight_specs(index_map):
    return [
        pl.BlockSpec((1, NB, NB, DB), index_map),
        pl.BlockSpec((1, NB, HB, NB), index_map),
        pl.BlockSpec((1, NB, NB, HB), index_map),
        pl.BlockSpec((1, NB, DB, NB), index_map),
    ]


def turned(factors):
    return tuple(jnp.swapaxes(w, -1, -2) for w in factors)


def shared_call(x_t, factors):
    return pl.pallas_call(
        shared_kernel,
        out_shape=jax.ShapeDtypeStruct((D, T), BF16),
        grid=(1,),
        in_specs=[pl.BlockSpec((D, T), lambda i: (0, 0))] + weight_specs(lambda i: (0, 0, 0, 0)),
        out_specs=pl.BlockSpec((D, T), lambda i: (0, 0)),
        scratch_shapes=[pltpu.VMEM((D, T), F32), pltpu.VMEM((D, T), F32)],
        compiler_params=pltpu.CompilerParams(vmem_limit_bytes=56 * 2**20),
        cost_estimate=pl.CostEstimate(flops=10**10, bytes_accessed=10**7, transcendentals=0),
        name="shared_expert",
    )(x_t, *factors)


def routed_call(counts, pos, slot_gates, x_all, factors, tiles):
    residents = pos.shape[0]
    sources = x_all.shape[0]
    grid_spec = pltpu.PrefetchScalarGridSpec(
        num_scalar_prefetch=1,
        grid=(residents, tiles),
        in_specs=[
            pl.BlockSpec((1, sources // 2, 1, 2 * T), lambda e, i, c: (e, 0, 0, 0)),
            pl.BlockSpec((1, 1, 1, T), lambda e, i, c: (e, i, 0, 0)),
            pl.BlockSpec((sources, D, T), lambda e, i, c: (0, 0, 0), pipeline_mode=pl.Buffered(1)),
        ]
        + weight_specs(lambda e, i, c: (e, 0, 0, 0)),
        out_specs=pl.BlockSpec((D, T), lambda e, i, c: (0, e * tiles + i)),
        scratch_shapes=[pltpu.VMEM((D, T), BF16), pltpu.VMEM((D, T), F32), pltpu.VMEM((D, T), F32)],
    )
    return pl.pallas_call(
        functools.partial(routed_kernel, tiles),
        out_shape=jax.ShapeDtypeStruct((D, residents * tiles * T), BF16),
        grid_spec=grid_spec,
        compiler_params=pltpu.CompilerParams(vmem_limit_bytes=62 * 2**20),
        cost_estimate=pl.CostEstimate(flops=4 * 10**10, bytes_accessed=2 * 10**7, transcendentals=0),
        name="routed_experts",
    )(counts, pos, slot_gates, x_all, *factors)


def combine_kernel(tiles, counts_ref, pos_ref, o_ref, y_ref, acc_ref):
    residents = counts_ref.shape[0]
    depth = tiles * T
    wanted = lax.broadcasted_iota(jnp.int32, (depth, 2 * T), 0)
    hots = [(wanted == pos_ref[e, 0, :, :]).astype(F32).astype(BF16) for e in range(residents)]
    hot = jnp.concatenate(hots, axis=0)
    step = 512

    def part(i, carry):
        rows = pl.ds(pl.multiple_of(i * step, step), step)
        total = jnp.dot(o_ref[rows, :], hot, preferred_element_type=F32).astype(BF16)
        y_ref[0, rows, :] = total[:, :T]
        y_ref[1, rows, :] = total[:, T:]
        return carry

    lax.fori_loop(0, D // step, part, 0)


def combine_call(counts, pos, outs, sources, tiles):
    residents = pos.shape[0]
    grid_spec = pltpu.PrefetchScalarGridSpec(
        num_scalar_prefetch=1,
        grid=(sources // 2,),
        in_specs=[
            pl.BlockSpec((residents, 1, 1, 2 * T), lambda s, c: (0, s, 0, 0)),
            pl.BlockSpec((D, residents * tiles * T), lambda s, c: (0, 0), pipeline_mode=pl.Buffered(1)),
        ],
        out_specs=pl.BlockSpec((2, D, T), lambda s, c: (s, 0, 0)),
        scratch_shapes=[pltpu.VMEM((8, T), F32)],
    )
    return pl.pallas_call(
        functools.partial(combine_kernel, tiles),
        out_shape=jax.ShapeDtypeStruct((sources, D, T), BF16),
        grid_spec=grid_spec,
        compiler_params=pltpu.CompilerParams(vmem_limit_bytes=48 * 2**20),
        name="combine",
    )(counts, pos, outs)


def grid_of(count):
    side = math.isqrt(count // 2)
    return count // side, side


def greet(z, y, nz, ny):
    barrier = pltpu.get_barrier_semaphore()
    for other in range(1, ny):
        pl.semaphore_signal(barrier, inc=1, device_id={"expert": z * ny + lax.rem(y + other, ny)})

    @pl.when(z > 0)
    def _():
        pl.semaphore_signal(barrier, inc=1, device_id={"expert": (z - 1) * ny + y})

    @pl.when(z < nz - 1)
    def _():
        pl.semaphore_signal(barrier, inc=1, device_id={"expert": (z + 1) * ny + y})

    peers = ny - 1 + jnp.where(z > 0, 1, 0) + jnp.where(z < nz - 1, 1, 0)
    pl.semaphore_wait(barrier, peers)


def gather_kernel(nz, x_ref, out_ref, own_sem, up_sem, down_sem, side_sem, recv_sem):
    ny = 2
    me = lax.axis_index("expert")
    z, y = me // ny, lax.rem(me, ny)
    beside = z * ny + (1 - y)

    def send(block, src, sem, target):
        return pltpu.make_async_remote_copy(
            src_ref=src, dst_ref=out_ref.at[block], send_sem=sem.at[block],
            recv_sem=recv_sem.at[block], device_id={"expert": target},
        )

    def arrived(block):
        send(block, out_ref.at[block], side_sem, beside).wait_recv()

    greet(z, y, nz, ny)
    own = pltpu.make_async_copy(x_ref, out_ref.at[me], own_sem)
    own.start()

    @pl.when(z < nz - 1)
    def _():
        send(me, x_ref, up_sem, me + ny).start()

    @pl.when(z > 0)
    def _():
        send(me, x_ref, down_sem, me - ny).start()

    send(me, x_ref, side_sem, beside).start()

    for k in range(1, nz):
        block = me - k * ny

        @pl.when(z >= k)
        def _():
            arrived(block)

            @pl.when(z < nz - 1)
            def _():
                send(block, out_ref.at[block], up_sem, me + ny).start()

            send(block, out_ref.at[block], side_sem, beside).start()

        later = me + k * ny

        @pl.when(z + k < nz)
        def _():
            arrived(later)

            @pl.when(z > 0)
            def _():
                send(later, out_ref.at[later], down_sem, me - ny).start()

            send(later, out_ref.at[later], side_sem, beside).start()

    for other in range(nz):
        arrived(other * ny + (1 - y))
    own.wait()
    for other in range(nz):
        block = other * ny + y
        send(block, out_ref.at[block], side_sem, beside).wait_send()

        @pl.when(jnp.logical_and(other <= z, z < nz - 1))
        def _():
            send(block, out_ref.at[block], up_sem, me + ny).wait_send()

        @pl.when(jnp.logical_and(other >= z, z > 0))
        def _():
            send(block, out_ref.at[block], down_sem, me - ny).wait_send()


def gather_tokens(x_t):
    count = lax.axis_size("expert")
    nz, ny = grid_of(count)
    if ny != 2:
        return lax.all_gather(x_t, "expert", axis=0, tiled=False)
    sems = pltpu.SemaphoreType.DMA((count,))
    return pl.pallas_call(
        functools.partial(gather_kernel, nz),
        out_shape=jax.ShapeDtypeStruct((count,) + x_t.shape, x_t.dtype),
        in_specs=[pl.BlockSpec(memory_space=pl.ANY)],
        out_specs=pl.BlockSpec(memory_space=pl.ANY),
        scratch_shapes=[pltpu.SemaphoreType.DMA, sems, sems, sems, sems],
        compiler_params=pltpu.CompilerParams(collective_id=0, has_side_effects=True),
        cost_estimate=pl.CostEstimate(flops=10**11, bytes_accessed=3 * 10**8, transcendentals=0),
        name="gather_tokens",
    )(x_t)


def scatter_kernel(
    nz, y_hbm, out_ref, held, beside_in, below_in, above_in,
    load_sem, side_sem, side_recv, up_sem, up_recv, down_sem, down_recv,
):
    ny = 2
    me = lax.axis_index("expert")
    z, y = me // ny, lax.rem(me, ny)
    beside = z * ny + (1 - y)

    def load(target):
        return pltpu.make_async_copy(y_hbm.at[target * ny + y], held.at[target], load_sem.at[target])

    def side(target):
        return pltpu.make_async_remote_copy(
            src_ref=y_hbm.at[target * ny + (1 - y)], dst_ref=beside_in.at[target],
            send_sem=side_sem.at[target], recv_sem=side_recv.at[target],
            device_id={"expert": beside},
        )

    def up(target):
        return pltpu.make_async_remote_copy(
            src_ref=held.at[target], dst_ref=below_in.at[target], send_sem=up_sem.at[target],
            recv_sem=up_recv.at[target], device_id={"expert": me + ny},
        )

    def down(target):
        return pltpu.make_async_remote_copy(
            src_ref=held.at[target], dst_ref=above_in.at[target], send_sem=down_sem.at[target],
            recv_sem=down_recv.at[target], device_id={"expert": me - ny},
        )

    def add(target, ref):
        step = 512

        def body(i, carry):
            rows = pl.ds(pl.multiple_of(i * step, step), step)
            total = held[target, rows, :].astype(F32) + ref[target, rows, :].astype(F32)
            held[target, rows, :] = total.astype(BF16)
            return carry

        lax.fori_loop(0, D // step, body, 0)

    greet(z, y, nz, ny)
    for k in range(nz - 1, -1, -1):
        @pl.when(z + k < nz)
        def _():
            side(z + k).start()

        if k > 0:
            @pl.when(z - k >= 0)
            def _():
                side(z - k).start()

    for target in range(nz):
        load(target).start()
    for target in range(nz):
        load(target).wait()
    for k in range(nz - 1, 0, -1):
        target = z + k

        @pl.when(z + k < nz)
        def _():
            side(target).wait_recv()
            add(target, beside_in)

            @pl.when(z > 0)
            def _():
                up(target).wait_recv()
                add(target, below_in)

            up(target).start()

        lower = z - k

        @pl.when(z - k >= 0)
        def _():
            side(lower).wait_recv()
            add(lower, beside_in)

            @pl.when(z < nz - 1)
            def _():
                down(lower).wait_recv()
                add(lower, above_in)

            down(lower).start()

    side(z).wait_recv()
    add(z, beside_in)

    @pl.when(z > 0)
    def _():
        up(z).wait_recv()
        add(z, below_in)

    @pl.when(z < nz - 1)
    def _():
        down(z).wait_recv()
        add(z, above_in)

    out_ref[...] = held[z]
    for target in range(nz):
        side(target).wait_send()

        @pl.when(target > z)
        def _():
            up(target).wait_send()

        @pl.when(target < z)
        def _():
            down(target).wait_send()


def scatter_sums(sums):
    count = lax.axis_size("expert")
    nz, ny = grid_of(count)
    if ny != 2:
        return lax.psum_scatter(sums, "expert", scatter_dimension=0, tiled=False)
    block = pltpu.VMEM((nz,) + sums.shape[1:], sums.dtype)
    sems = pltpu.SemaphoreType.DMA((nz,))
    return pl.pallas_call(
        functools.partial(scatter_kernel, nz),
        out_shape=jax.ShapeDtypeStruct(sums.shape[1:], sums.dtype),
        in_specs=[pl.BlockSpec(memory_space=pl.ANY)],
        out_specs=pl.BlockSpec(memory_space=pltpu.VMEM),
        scratch_shapes=[block] * 4 + [sems] * 7,
        compiler_params=pltpu.CompilerParams(
            collective_id=1, has_side_effects=True, vmem_limit_bytes=40 * 2**20
        ),
        cost_estimate=pl.CostEstimate(flops=10**11, bytes_accessed=3 * 10**8, transcendentals=0),
        name="scatter_sums",
    )(sums)


def shards(tokens, expert_ids, gate_codes, *factors):
    shared, routed = factors[:4], factors[4:]
    residents = routed[0].shape[0]
    sources = lax.axis_size("expert")
    tok_rows = tokens.shape[0]
    experts_all = residents * sources
    capacity = max(2, 6 * tok_rows // experts_all)
    tiles = -(-sources * capacity // T)

    x_t = tokens.T
    x_all = gather_tokens(x_t)
    codes = gate_codes.astype(F32)
    gates = codes / jnp.sum(codes, axis=1, keepdims=True)
    ids_all = lax.all_gather(expert_ids.T, "expert", axis=0)
    gates_all = lax.all_gather(gates.T, "expert", axis=0)
    mine = lax.axis_index("expert") * residents + jnp.arange(residents, dtype=jnp.int32)
    match = ids_all[None] == mine[:, None, None, None]
    picked = jnp.any(match, axis=2).reshape(residents, sources * tok_rows)
    gate = jnp.sum(jnp.where(match, gates_all[None], 0.0), axis=2).reshape(residents, sources * tok_rows)
    ones = picked.astype(jnp.int32)
    ranks = jnp.cumsum(ones, axis=1)
    counts = ranks[:, -1]
    pos = jnp.where(picked, ranks - 1, -1)
    slots = jnp.arange(tiles * T, dtype=jnp.int32)
    slot_gates = jnp.sum(
        jnp.where(pos[:, None, :] == slots[None, :, None], gate[:, None, :], 0.0), axis=2
    ).reshape(residents, tiles, 1, T)
    pos = pos.reshape(residents, sources // 2, 1, 2 * T)

    outs = routed_call(counts, pos, slot_gates, x_all, turned(routed), tiles)
    y = combine_call(counts, pos, outs, sources, tiles)
    sums = scatter_sums(y)
    whole = tuple(lax.all_gather(w, "dp", axis=0, tiled=True)[None] for w in turned(shared))
    shared_t = shared_call(x_t, whole)
    total = shared_t.astype(F32) + sums.astype(F32)
    return total.astype(BF16).T


def solution(mesh):
    in_specs = (
        P(("expert", "dp"), None),
        P(("expert", "dp"), None),
        P(("expert", "dp"), None),
        P("dp", None, None),
        P("dp", None, None),
        P("dp", None, None),
        P("dp", None, None),
        P("expert", None, None, None),
        P("expert", None, None, None),
        P("expert", None, None, None),
        P("expert", None, None, None),
    )
    out_specs = P(("expert", "dp"), None)
    return jax.shard_map(shards, mesh=mesh, in_specs=in_specs, out_specs=out_specs, check_vma=False)
```

```python
import functools
import math

import jax
import jax.numpy as jnp
from jax import lax
from jax.experimental import pallas as pl
from jax.experimental.pallas import tpu as pltpu
from jax.sharding import PartitionSpec as P

D = 4096
NB = 64
DB = 64
HB = 256
T = 128
F32 = jnp.float32
BF16 = jnp.bfloat16


def tile_monarch(x_ref, lanes, w1_ref, w2_ref, w3_ref, w4_ref, z_refs, u_refs, store):
    def spread(refs, rows, value):
        for i in range(lanes):
            refs[i][rows, :] = value[:, i * T : (i + 1) * T]

    def strided(refs, start):
        parts = [refs[i][pl.ds(start, NB, stride=NB), :] for i in range(lanes)]
        return jnp.concatenate(parts, axis=1).astype(BF16)

    def up(a, carry):
        rows = pl.ds(pl.multiple_of(a * DB, DB), DB)
        x = x_ref[rows, : lanes * T]
        spread(z_refs, rows, jnp.dot(w1_ref[0, a], x, preferred_element_type=F32))
        return carry

    lax.fori_loop(0, NB, up, 0, unroll=8)

    def middle(j, carry):
        hidden = jnp.dot(w2_ref[0, j], strided(z_refs, j), preferred_element_type=F32)
        hidden = (0.5 * hidden) * (1.0 + lax.erf(hidden * (0.5**0.5)))
        u = jnp.dot(w3_ref[0, j], hidden.astype(BF16), preferred_element_type=F32)
        spread(u_refs, pl.ds(pl.multiple_of(j * NB, NB), NB), u)
        return carry

    lax.fori_loop(0, NB, middle, 0, unroll=4)

    def down(k, carry):
        rows = pl.ds(pl.multiple_of(k * DB, DB), DB)
        store(rows, jnp.dot(w4_ref[0, k], strided(u_refs, k), preferred_element_type=F32))
        return carry

    lax.fori_loop(0, NB, down, 0, unroll=8)


def shared_kernel(x_ref, w1_ref, w2_ref, w3_ref, w4_ref, o_ref, z_ref, u_ref):
    def store(rows, value):
        o_ref[rows, :] = value.astype(BF16)

    tile_monarch(x_ref, 1, w1_ref, w2_ref, w3_ref, w4_ref, (z_ref,), (u_ref,), store)


def routed_kernel(
    counts_ref, pos_ref, gate_ref, x_ref, w1_ref, w2_ref, w3_ref, w4_ref,
    o_ref, x_scr, z0_ref, z1_ref, u0_ref, u1_ref,
):
    expert, tile = pl.program_id(0), pl.program_id(1)
    left = counts_ref[expert] - tile * 2 * T
    sources = x_ref.shape[0]

    @pl.when(left <= T)
    def _():
        o_ref[...] = jnp.zeros_like(o_ref)

    def serve(lanes):
        width = lanes * T
        wanted = lax.broadcasted_iota(jnp.int32, (width, 2 * T), 0) + tile * 2 * T
        step = D // 8

        for part in range(8):
            rows = pl.ds(part * step, step)

            def pick(pair, total):
                both = jnp.concatenate([x_ref[2 * pair, rows, :], x_ref[2 * pair + 1, rows, :]], axis=1)
                onehot = (wanted == pos_ref[0, pair, :, :]).astype(F32).astype(BF16)
                return total + lax.dot_general(
                    both, onehot, (((1,), (1,)), ((), ())), preferred_element_type=F32
                )

            total = lax.fori_loop(0, sources // 2, pick, jnp.zeros((step, width), F32))
            x_scr[rows, :width] = total.astype(BF16)

        gate = gate_ref[0, 0][:, :width]

        def store(rows, value):
            o_ref[rows, :width] = (value * gate).astype(BF16)

        tile_monarch(
            x_scr, lanes, w1_ref, w2_ref, w3_ref, w4_ref, (z0_ref, z1_ref), (u0_ref, u1_ref), store
        )

    @pl.when(left > T)
    def _():
        serve(2)

    @pl.when(jnp.logical_and(left > 0, left <= T))
    def _():
        serve(1)


def weight_specs(index_map, buffers=2):
    shapes = ((NB, DB), (HB, NB), (NB, HB), (DB, NB))
    mode = pl.Buffered(buffers)
    return [pl.BlockSpec((1, NB) + shape, index_map, pipeline_mode=mode) for shape in shapes]


def turned(factors):
    return tuple(jnp.swapaxes(w, -1, -2) for w in factors)


def shared_call(x_t, factors):
    return pl.pallas_call(
        shared_kernel,
        out_shape=jax.ShapeDtypeStruct((D, T), BF16),
        grid=(1,),
        in_specs=[pl.BlockSpec((D, T), lambda i: (0, 0))] + weight_specs(lambda i: (0, 0, 0, 0)),
        out_specs=pl.BlockSpec((D, T), lambda i: (0, 0)),
        scratch_shapes=[pltpu.VMEM((D, T), F32), pltpu.VMEM((D, T), F32)],
        compiler_params=pltpu.CompilerParams(vmem_limit_bytes=56 * 2**20),
        cost_estimate=pl.CostEstimate(flops=10**10, bytes_accessed=10**7, transcendentals=0),
        name="shared_expert",
    )(x_t, *factors)


def routed_call(counts, pos, slot_gates, x_all, factors, tiles):
    residents = pos.shape[0]
    sources = x_all.shape[0]
    grid_spec = pltpu.PrefetchScalarGridSpec(
        num_scalar_prefetch=1,
        grid=(residents, tiles),
        in_specs=[
            pl.BlockSpec((1, sources // 2, 1, 2 * T), lambda e, i, c: (e, 0, 0, 0)),
            pl.BlockSpec((1, 1, 1, 2 * T), lambda e, i, c: (e, i, 0, 0)),
            pl.BlockSpec((sources, x_all.shape[1], T), lambda e, i, c: (0, 0, 0), pipeline_mode=pl.Buffered(1)),
        ]
        + weight_specs(lambda e, i, c: (e, 0, 0, 0), 2 if sources <= 8 else 1),
        out_specs=pl.BlockSpec((D, 2 * T), lambda e, i, c: (0, e * tiles + i)),
        scratch_shapes=[pltpu.VMEM((D, 2 * T), BF16)] + [pltpu.VMEM((D, T), F32)] * 4,
    )
    return pl.pallas_call(
        routed_kernel,
        out_shape=jax.ShapeDtypeStruct((D, residents * tiles * 2 * T), BF16),
        grid_spec=grid_spec,
        compiler_params=pltpu.CompilerParams(vmem_limit_bytes=62 * 2**20),
        cost_estimate=pl.CostEstimate(flops=4 * 10**10, bytes_accessed=2 * 10**7, transcendentals=0),
        name="routed_experts",
    )(counts, pos, slot_gates, x_all, *factors)


def combine_kernel(depth, window, starts_ref, pos_ref, o_ref, y_ref):
    residents = starts_ref.shape[0]
    pair = pl.program_id(0)
    wanted = lax.broadcasted_iota(jnp.int32, (window, 2 * T), 0)
    begins = [pl.multiple_of(starts_ref[e, pair] * T, T) for e in range(residents)]
    hots = [
        (wanted + begins[e] == pos_ref[e, 0, :, :]).astype(F32).astype(BF16) for e in range(residents)
    ]
    hot = jnp.concatenate(hots, axis=0)
    step = 512

    def part(i, carry):
        rows = pl.ds(pl.multiple_of(i * step, step), step)
        near = [
            o_ref[rows, pl.ds(pl.multiple_of(begins[e] + e * depth, T), window)] for e in range(residents)
        ]
        total = jnp.dot(jnp.concatenate(near, axis=1), hot, preferred_element_type=F32).astype(BF16)
        y_ref[0, rows, :] = total[:, :T]
        y_ref[1, rows, :] = total[:, T:]
        return carry

    lax.fori_loop(0, D // step, part, 0)


def combine_call(starts, pos, outs, sources, depth, window):
    residents = pos.shape[0]
    grid_spec = pltpu.PrefetchScalarGridSpec(
        num_scalar_prefetch=1,
        grid=(sources // 2,),
        in_specs=[
            pl.BlockSpec((residents, 1, 1, 2 * T), lambda s, c: (0, s, 0, 0)),
            pl.BlockSpec((D, residents * depth), lambda s, c: (0, 0), pipeline_mode=pl.Buffered(1)),
        ],
        out_specs=pl.BlockSpec((2, D, T), lambda s, c: (s, 0, 0)),
    )
    return pl.pallas_call(
        functools.partial(combine_kernel, depth, window),
        out_shape=jax.ShapeDtypeStruct((sources, D, T), BF16),
        grid_spec=grid_spec,
        compiler_params=pltpu.CompilerParams(vmem_limit_bytes=48 * 2**20),
        name="combine",
    )(starts, pos, outs)


def grid_of(count):
    side = math.isqrt(count // 2)
    return count // side, side


def greet(z, y, nz, ny):
    barrier = pltpu.get_barrier_semaphore()
    for other in range(1, ny):
        pl.semaphore_signal(barrier, inc=1, device_id={"expert": z * ny + lax.rem(y + other, ny)})

    @pl.when(z > 0)
    def _():
        pl.semaphore_signal(barrier, inc=1, device_id={"expert": (z - 1) * ny + y})

    @pl.when(z < nz - 1)
    def _():
        pl.semaphore_signal(barrier, inc=1, device_id={"expert": (z + 1) * ny + y})

    peers = ny - 1 + jnp.where(z > 0, 1, 0) + jnp.where(z < nz - 1, 1, 0)
    pl.semaphore_wait(barrier, peers)


def gather_kernel(nz, x_ref, out_ref, own_sem, up_sem, down_sem, side_sem, recv_sem):
    ny = 2
    me = lax.axis_index("expert")
    z, y = me // ny, lax.rem(me, ny)
    beside = z * ny + (1 - y)

    def send(block, src, sem, target):
        return pltpu.make_async_remote_copy(
            src_ref=src, dst_ref=out_ref.at[block], send_sem=sem.at[block],
            recv_sem=recv_sem.at[block], device_id={"expert": target},
        )

    def arrived(block):
        send(block, out_ref.at[block], side_sem, beside).wait_recv()

    greet(z, y, nz, ny)
    own = pltpu.make_async_copy(x_ref, out_ref.at[me], own_sem)
    own.start()

    @pl.when(z < nz - 1)
    def _():
        send(me, x_ref, up_sem, me + ny).start()

    @pl.when(z > 0)
    def _():
        send(me, x_ref, down_sem, me - ny).start()

    send(me, x_ref, side_sem, beside).start()

    for k in range(1, nz):
        block = me - k * ny

        @pl.when(z >= k)
        def _():
            arrived(block)

            @pl.when(z < nz - 1)
            def _():
                send(block, out_ref.at[block], up_sem, me + ny).start()

            send(block, out_ref.at[block], side_sem, beside).start()

        later = me + k * ny

        @pl.when(z + k < nz)
        def _():
            arrived(later)

            @pl.when(z > 0)
            def _():
                send(later, out_ref.at[later], down_sem, me - ny).start()

            send(later, out_ref.at[later], side_sem, beside).start()

    for other in range(nz):
        arrived(other * ny + (1 - y))
    own.wait()
    for other in range(nz):
        block = other * ny + y
        send(block, out_ref.at[block], side_sem, beside).wait_send()

        @pl.when(jnp.logical_and(other <= z, z < nz - 1))
        def _():
            send(block, out_ref.at[block], up_sem, me + ny).wait_send()

        @pl.when(jnp.logical_and(other >= z, z > 0))
        def _():
            send(block, out_ref.at[block], down_sem, me - ny).wait_send()


def gather_tokens(x_t):
    count = lax.axis_size("expert")
    nz, ny = grid_of(count)
    if ny != 2:
        return lax.all_gather(x_t, "expert", axis=0, tiled=False)
    sems = pltpu.SemaphoreType.DMA((count,))
    return pl.pallas_call(
        functools.partial(gather_kernel, nz),
        out_shape=jax.ShapeDtypeStruct((count,) + x_t.shape, x_t.dtype),
        in_specs=[pl.BlockSpec(memory_space=pl.ANY)],
        out_specs=pl.BlockSpec(memory_space=pl.ANY),
        scratch_shapes=[pltpu.SemaphoreType.DMA, sems, sems, sems, sems],
        compiler_params=pltpu.CompilerParams(collective_id=0, has_side_effects=True),
        cost_estimate=pl.CostEstimate(flops=10**11, bytes_accessed=3 * 10**8, transcendentals=0),
        name="gather_tokens",
    )(x_t)


def scatter_kernel(
    nz, y_hbm, out_ref, held, beside_in, below_in, above_in,
    load_sem, side_sem, side_recv, up_sem, up_recv, down_sem, down_recv,
):
    ny = 2
    me = lax.axis_index("expert")
    z, y = me // ny, lax.rem(me, ny)
    beside = z * ny + (1 - y)

    def load(target):
        return pltpu.make_async_copy(y_hbm.at[target * ny + y], held.at[target], load_sem.at[target])

    def side(target):
        return pltpu.make_async_remote_copy(
            src_ref=y_hbm.at[target * ny + (1 - y)], dst_ref=beside_in.at[target],
            send_sem=side_sem.at[target], recv_sem=side_recv.at[target],
            device_id={"expert": beside},
        )

    def up(target):
        return pltpu.make_async_remote_copy(
            src_ref=held.at[target], dst_ref=below_in.at[target], send_sem=up_sem.at[target],
            recv_sem=up_recv.at[target], device_id={"expert": me + ny},
        )

    def down(target):
        return pltpu.make_async_remote_copy(
            src_ref=held.at[target], dst_ref=above_in.at[target], send_sem=down_sem.at[target],
            recv_sem=down_recv.at[target], device_id={"expert": me - ny},
        )

    def add(target, ref):
        step = 512

        def body(i, carry):
            rows = pl.ds(pl.multiple_of(i * step, step), step)
            total = held[target, rows, :].astype(F32) + ref[target, rows, :].astype(F32)
            held[target, rows, :] = total.astype(BF16)
            return carry

        lax.fori_loop(0, D // step, body, 0)

    greet(z, y, nz, ny)
    for k in range(nz - 1, -1, -1):
        @pl.when(z + k < nz)
        def _():
            side(z + k).start()

        if k > 0:
            @pl.when(z - k >= 0)
            def _():
                side(z - k).start()

    for target in range(nz):
        load(target).start()
    for target in range(nz):
        load(target).wait()
    for k in range(nz - 1, 0, -1):
        target = z + k

        @pl.when(z + k < nz)
        def _():
            side(target).wait_recv()
            add(target, beside_in)

            @pl.when(z > 0)
            def _():
                up(target).wait_recv()
                add(target, below_in)

            up(target).start()

        lower = z - k

        @pl.when(z - k >= 0)
        def _():
            side(lower).wait_recv()
            add(lower, beside_in)

            @pl.when(z < nz - 1)
            def _():
                down(lower).wait_recv()
                add(lower, above_in)

            down(lower).start()

    side(z).wait_recv()
    add(z, beside_in)

    @pl.when(z > 0)
    def _():
        up(z).wait_recv()
        add(z, below_in)

    @pl.when(z < nz - 1)
    def _():
        down(z).wait_recv()
        add(z, above_in)

    out_ref[...] = held[z]
    for target in range(nz):
        side(target).wait_send()

        @pl.when(target > z)
        def _():
            up(target).wait_send()

        @pl.when(target < z)
        def _():
            down(target).wait_send()


def scatter_sums(sums):
    count = lax.axis_size("expert")
    nz, ny = grid_of(count)
    if ny != 2:
        return lax.psum_scatter(sums, "expert", scatter_dimension=0, tiled=False)
    block = pltpu.VMEM((nz,) + sums.shape[1:], sums.dtype)
    sems = pltpu.SemaphoreType.DMA((nz,))
    return pl.pallas_call(
        functools.partial(scatter_kernel, nz),
        out_shape=jax.ShapeDtypeStruct(sums.shape[1:], sums.dtype),
        in_specs=[pl.BlockSpec(memory_space=pl.ANY)],
        out_specs=pl.BlockSpec(memory_space=pltpu.VMEM),
        scratch_shapes=[block] * 4 + [sems] * 7,
        compiler_params=pltpu.CompilerParams(
            collective_id=1, has_side_effects=True, vmem_limit_bytes=40 * 2**20
        ),
        cost_estimate=pl.CostEstimate(flops=10**11, bytes_accessed=3 * 10**8, transcendentals=0),
        name="scatter_sums",
    )(sums)


def shards(tokens, expert_ids, gate_codes, *factors):
    shared, routed = factors[:4], factors[4:]
    residents = routed[0].shape[0]
    sources = lax.axis_size("expert")
    tok_rows = tokens.shape[0]
    experts_all = residents * sources
    capacity = max(2, 6 * tok_rows // experts_all)
    tiles = -(-sources * capacity // (2 * T))
    depth = tiles * 2 * T
    window = min(depth, -(-(T - 1 + 2 * capacity) // T) * T)

    extra = jnp.concatenate([expert_ids, gate_codes], axis=1).T.astype(BF16)
    extra = jnp.pad(extra, ((0, 16 - extra.shape[0]), (0, 0)))
    x_t = jnp.concatenate([tokens.T, extra], axis=0)
    x_all = gather_tokens(x_t)
    ids_all = x_all[:, D : D + 2].astype(jnp.int32)
    codes = x_all[:, D + 2 : D + 4].astype(F32)
    gates_all = codes / jnp.sum(codes, axis=1, keepdims=True)
    mine = lax.axis_index("expert") * residents + jnp.arange(residents, dtype=jnp.int32)
    match = ids_all[None] == mine[:, None, None, None]
    picked = jnp.any(match, axis=2).reshape(residents, sources * tok_rows)
    gate = jnp.sum(jnp.where(match, gates_all[None], 0.0), axis=2).reshape(residents, sources * tok_rows)
    ones = picked.astype(jnp.int32)
    ranks = jnp.cumsum(ones, axis=1)
    counts = ranks[:, -1]
    starts = (ranks - ones).reshape(residents, sources // 2, 2 * T)[:, :, 0]
    starts = jnp.minimum(starts, depth - window) // T
    pos = jnp.where(picked, ranks - 1, -1)
    slots = jnp.arange(depth, dtype=jnp.int32)
    slot_gates = jnp.sum(
        jnp.where(pos[:, None, :] == slots[None, :, None], gate[:, None, :], 0.0), axis=2
    ).reshape(residents, tiles, 1, 2 * T)
    pos = pos.reshape(residents, sources // 2, 1, 2 * T)

    outs = routed_call(counts, pos, slot_gates, x_all, turned(routed), tiles)
    y = combine_call(starts, pos, outs, sources, depth, window)
    sums = scatter_sums(y)
    whole = tuple(lax.all_gather(w, "dp", axis=0, tiled=True)[None] for w in turned(shared))
    shared_t = shared_call(x_t, whole)
    total = shared_t.astype(F32) + sums.astype(F32)
    return total.astype(BF16).T


def solution(mesh):
    in_specs = (
        P(("expert", "dp"), None),
        P(("expert", "dp"), None),
        P(("expert", "dp"), None),
        P("dp", None, None),
        P("dp", None, None),
        P("dp", None, None),
        P("dp", None, None),
        P("expert", None, None, None),
        P("expert", None, None, None),
        P("expert", None, None, None),
        P("expert", None, None, None),
    )
    out_specs = P(("expert", "dp"), None)
    return jax.shard_map(shards, mesh=mesh, in_specs=in_specs, out_specs=out_specs, check_vma=False)
```
